256 devices in a mesh: node: 32 (over z_hi, x, core), ctrl: 8 (over y, z_lo).
Axes of the slice: x: 4, y: 4, z: 8 (z_hi: 4, z_lo: 2; z = z_hi * 2 + z_lo), core: 2. Of those that a mesh axis runs over, the one named last changes fastest.
Arguments:
- sensitivity: bfloat16 [96, 131072], P(None, 'node'), may hold values from -1 to 1
- node_xyz: float32 [3, 131072], P(None, 'node'), may hold values from 0 to 1
- ctrl_xyz: float32 [3, 16384], P(None, 'ctrl'), may hold values from 0 to 1
- inverse: bfloat16 [16384, 16384], P('ctrl', 'node'), may hold values from -0.046875 to 0.046875
Outputs:
- control_grad: float32 [96, 16384], P(None, ('node', 'ctrl'))
The draws below stay inside these ranges and needn't reach their ends.
All inputs are finite; a program needn't handle non-finite values.
Results may differ from the reference program's by a relative error of at most 0.004.
Values may be sent and summed in bfloat16 or wider, within the bound.
No kernel may reach another device: no remote copies, remote signals or barrier semaphores. Data moves between devices by JAX's collectives and lax.ppermute only.
A program may use at most 64 MiB of HBM per device.

```python
import jax
import jax.numpy as jnp
from jax import lax

OBJ = 32
NC = 16384
NODES = 131072


def level_of(key, shape, shards, least, largest):
    gain = 1.0
    for position, blocks in shards:
        heights = jax.random.uniform(jax.random.fold_in(jax.random.fold_in(key, 6), position), (blocks,), jnp.float32, least / len(shards), largest / len(shards))
        gain = gain * jnp.repeat(jnp.exp(heights), shape[position] // blocks).reshape((-1,) + (1,) * (len(shape) - 1 - position))
    return gain


def scatter_about(stream_key, shape, width, most, shards=(), held_as=jnp.bfloat16):
    values = jax.random.normal(stream_key, shape, jnp.float32) * width
    if len(shards) > 0:
        values = level_of(stream_key, shape, shards, -0.22, 0.18) * values
    return jnp.clip(values, min=-most, max=most).astype(held_as)


def setup_inputs(seed: int = 0) -> dict:
    key_of = jax.random.split(jax.random.key(seed), 5)
    sensitivity = scatter_about(key_of[0], (3 * OBJ, NODES), (max(NODES // 4096, 1)) ** -0.5, 1.0, ((1, 32),))
    node_xyz = jnp.clip(1.0 * jax.random.uniform(key_of[1], (3, NODES), jnp.float32) ** level_of(key_of[1], (3, NODES), ((1, 32),), -0.2, 0.2), 0.0, 1.0)
    ctrl_xyz = jnp.clip(1.0 * jax.random.uniform(key_of[2], (3, NC), jnp.float32) ** level_of(key_of[2], (3, NC), ((1, 8),), -0.2, 0.2), 0.0, 1.0)
    inverse = scatter_about(key_of[3], (NC, NC), NC ** -0.5, 0.046875, ((0, 8), (1, 32)))
    return {"sensitivity": sensitivity, "node_xyz": node_xyz, "ctrl_xyz": ctrl_xyz, "inverse": inverse}


support_radius = 0.12

def kernel_tile(node_part, ctrl_xyz):
    delta_x = node_part[0][:, None] - ctrl_xyz[0][None, :]
    delta_y = node_part[1][:, None] - ctrl_xyz[1][None, :]
    delta_z = node_part[2][:, None] - ctrl_xyz[2][None, :]
    scaled = jnp.sqrt(delta_x * delta_x + delta_y * delta_y + delta_z * delta_z) / support_radius
    remain = jnp.maximum(1.0 - scaled, 0.0)
    return (remain ** 4 * (4.0 * scaled + 1.0)).astype(jnp.bfloat16)

def reference(sensitivity, node_xyz, ctrl_xyz, inverse):
    nodes_all = node_xyz.shape[1]
    span_rows = min(1024, nodes_all)
    steps_count = nodes_all // span_rows

    def advance(running, number):
        offset = (number * span_rows).astype(jnp.int32)
        node_part = lax.dynamic_slice_in_dim(node_xyz, offset, span_rows, 1)
        sens_part = lax.dynamic_slice_in_dim(sensitivity, offset, span_rows, 1)
        weights_tile = kernel_tile(node_part, ctrl_xyz)
        return (running + jnp.dot(sens_part, weights_tile, preferred_element_type=jnp.float32), None)
    start_sum = jnp.zeros((sensitivity.shape[0], ctrl_xyz.shape[1]), jnp.float32)
    pulled, _ = lax.scan(advance, start_sum, jnp.arange(steps_count, dtype=jnp.int32))
    pulled_low = pulled.astype(jnp.bfloat16)
    return jnp.dot(pulled_low, inverse, preferred_element_type=jnp.float32)
```

```python
import functools

import jax
import jax.numpy as jnp
from jax import lax
from jax.experimental import pallas as pl
from jax.experimental.pallas import tpu as pltpu
from jax.sharding import Mesh, PartitionSpec as P

support_radius = 0.12
stretch = 4.0 / support_radius
depth = 128
span = 256


def pieces_of(values):
    high = values.astype(jnp.bfloat16).astype(jnp.float32)
    rest = values - high
    middle = rest.astype(jnp.bfloat16).astype(jnp.float32)
    low = (rest - middle).astype(jnp.bfloat16).astype(jnp.float32)
    return high, middle, low


def write_features(xyz_ref, rows, is_node):
    count = xyz_ref.shape[1]
    place = (xyz_ref[...] - 0.5) * stretch
    norm = (
        place[0:1] * place[0:1] + place[1:2] * place[1:2] + place[2:3] * place[2:3]
    )
    parts = pieces_of(place)
    norm_parts = pieces_of(norm)
    ones = jnp.ones((3, count), jnp.float32)
    rows[...] = jnp.zeros_like(rows)
    for i in range(3):
        for j in range(3):
            k = 3 * (3 * i + j)
            rows[k : k + 3, :] = parts[i] if is_node else -2.0 * parts[j]
    norm_at, ones_at = (27, 30) if is_node else (30, 27)
    rows[ones_at : ones_at + 3, :] = ones
    for i in range(3):
        rows[norm_at + i : norm_at + i + 1, :] = norm_parts[i]


def features_kernel(node_ref, ctrl_ref, node_out, ctrl_out, node_rows, ctrl_rows):
    write_features(node_ref, node_rows, True)
    write_features(ctrl_ref, ctrl_rows, False)
    ctrl_out[...] = ctrl_rows[...].astype(jnp.bfloat16)
    node_out[...] = node_rows[...].T.astype(jnp.bfloat16)


def features(node_xyz, ctrl_xyz):
    nodes, ctrls = node_xyz.shape[1], ctrl_xyz.shape[1]
    return pl.pallas_call(
        features_kernel,
        out_shape=[
            jax.ShapeDtypeStruct((nodes, depth), jnp.bfloat16),
            jax.ShapeDtypeStruct((depth, ctrls), jnp.bfloat16),
        ],
        scratch_shapes=[
            pltpu.VMEM((depth, nodes), jnp.float32),
            pltpu.VMEM((depth, ctrls), jnp.float32),
        ],
        cost_estimate=pl.CostEstimate(
            flops=nodes * 1000, bytes_accessed=nodes * 512, transcendentals=0
        ),
        name="features",
    )(node_xyz, ctrl_xyz)


def wendland(squared):
    squared = jnp.maximum(squared, 1e-30)
    r4 = squared * lax.rsqrt(squared)
    remain = jnp.maximum(4.0 - r4, 0.0)
    remain2 = remain * remain
    return (remain2 * remain2 * (r4 + 1.0)).astype(jnp.bfloat16)


def pull_kernel(tile, has_add, index_ref, node_ref, ctrl_ref, sens_ref, *rest):
    out_ref = rest[-1]
    nodes = node_ref.shape[0]

    def body(i, acc):
        at = pl.multiple_of(i * tile, tile)
        squared = jnp.dot(
            node_ref[pl.ds(at, tile), :],
            ctrl_ref[...],
            preferred_element_type=jnp.float32,
        )
        return acc + jnp.dot(
            sens_ref[:, pl.ds(at, tile)],
            wendland(squared),
            preferred_element_type=jnp.float32,
        )

    acc = lax.fori_loop(0, nodes // tile, body, jnp.zeros(out_ref.shape, jnp.float32))
    acc = acc * (1.0 / 256.0)
    if has_add:
        acc = acc + rest[0][...]
    out_ref[...] = acc


def pull(index, blocks, node_feat, ctrl_feat, sens, add=None, tile=2048):
    nodes = node_feat.shape[0]
    rows = sens.shape[0]
    in_specs = [
        pl.BlockSpec((nodes, depth), lambda i, idx: (0, 0)),
        pl.BlockSpec((depth, span), lambda i, idx: (0, idx[i])),
        pl.BlockSpec((rows, nodes), lambda i, idx: (0, 0)),
    ]
    args = [node_feat, ctrl_feat, sens]
    if add is not None:
        in_specs.append(pl.BlockSpec((rows, span), lambda i, idx: (0, idx[blocks])))
        args.append(add)
    return pl.pallas_call(
        functools.partial(pull_kernel, tile, add is not None),
        out_shape=jax.ShapeDtypeStruct((rows, blocks * span), jnp.float32),
        grid_spec=pltpu.PrefetchScalarGridSpec(
            num_scalar_prefetch=1,
            grid=(blocks,),
            in_specs=in_specs,
            out_specs=pl.BlockSpec((rows, span), lambda i, idx: (0, i)),
        ),
        cost_estimate=pl.CostEstimate(
            flops=blocks * span * nodes * 400,
            bytes_accessed=nodes * 448,
            transcendentals=blocks * span * nodes,
        ),
        name="pull",
    )(index, *args)


def product_kernel(index_ref, *refs):
    blocks, inverse_ref, out_ref = refs[:-2], refs[-2], refs[-1]
    total = None
    for i, block in enumerate(blocks):
        half = block.shape[1]
        at = pl.multiple_of(index_ref[i] * half, half)
        term = jnp.dot(
            block[...],
            inverse_ref[pl.ds(at, half), :],
            preferred_element_type=jnp.float32,
        )
        total = term if total is None else total + term
    shares, rows, lanes = out_ref.shape
    width = lanes // 2
    for j in range(shares):
        share = total[:, j * width : (j + 1) * width]
        out_ref[j] = jnp.concatenate([share[:rows], share[rows:]], axis=1).astype(
            out_ref.dtype
        )


def product(index, blocks, inverse, shares):
    rows, width = blocks[0].shape[0], inverse.shape[1] // shares
    count = len(blocks)
    whole = pl.BlockSpec(memory_space=pltpu.VMEM)
    return pl.pallas_call(
        product_kernel,
        out_shape=jax.ShapeDtypeStruct((shares, rows // 2, 2 * width), jnp.bfloat16),
        in_specs=[pl.BlockSpec(memory_space=pltpu.SMEM)] + [whole] * (count + 1),
        out_specs=whole,
        name="product",
    )(index, *blocks, inverse)


def finish_kernel(shares_ref, out_ref):
    total = shares_ref[0].astype(jnp.float32)
    for j in range(1, shares_ref.shape[0]):
        total = total + shares_ref[j].astype(jnp.float32)
    rows, lanes = total.shape
    out_ref[0:rows, :] = total[:, : lanes // 2]
    out_ref[rows:, :] = total[:, lanes // 2 :]


def finish(shares):
    _, rows, lanes = shares.shape
    return pl.pallas_call(
        finish_kernel,
        out_shape=jax.ShapeDtypeStruct((2 * rows, lanes // 2), jnp.float32),
        name="finish",
    )(shares)


def shifted(value, axis, by):
    size = lax.axis_size(axis)
    return lax.ppermute(value, axis, [(i, (i + by) % size) for i in range(size)])


def per_device(sensitivity, node_xyz, ctrl_xyz, inverse):
    core = lax.axis_index("core").astype(jnp.int32)
    x = lax.axis_index("x").astype(jnp.int32)
    node_feat, ctrl_feat = features(node_xyz, ctrl_xyz)

    own = core * 4
    other = (1 - core) * 4
    other_index = other + jnp.arange(5, dtype=jnp.int32) % 4
    for_other = pull(other_index, 4, node_feat, ctrl_feat, sensitivity)
    from_other = shifted(for_other, "core", 1)

    def quarter(by, add):
        which = (x + by) % 4
        index = jnp.stack([own + which, which])
        return pull(index, 1, node_feat, ctrl_feat, sensitivity, add)

    arrived = []
    for by in (2, 1, 3):
        arrived.append(shifted(quarter(by, from_other), "x", by))
    summed = quarter(0, from_other) + arrived[0] + arrived[1] + arrived[2]

    low = summed.astype(jnp.bfloat16)
    for by in (2, 1, 3):
        summed = summed + shifted(low, "zh", by).astype(jnp.float32)
    mine = summed.astype(jnp.bfloat16)

    along_x = [mine] + [shifted(mine, "x", by) for by in (2, 1, 3)]
    index_x = [(x - by) % 4 for by in (0, 2, 1, 3)]
    joined = jnp.concatenate(along_x, axis=1)
    swapped = shifted(joined, "core", 1)
    both = [b for b in along_x] + [
        swapped[:, i * span : (i + 1) * span] for i in range(4)
    ]
    index = jnp.stack([own + i for i in index_x] + [other + i for i in index_x])
    shares = product(index, both, inverse, 8)
    arrived_shares = lax.all_to_all(
        shares, ("y", "zl"), split_axis=0, concat_axis=0, tiled=True
    )
    return finish(arrived_shares)


def solution(mesh):
    fine = Mesh(
        mesh.devices.reshape(4, 4, 2, 4, 2), ("zh", "x", "core", "y", "zl")
    )
    node, ctrl = ("zh", "x", "core"), ("y", "zl")
    in_specs = (P(None, node), P(None, node), P(None, ctrl), P(ctrl, node))
    out_specs = P(None, node + ctrl)
    return jax.shard_map(
        per_device, mesh=fine, in_specs=in_specs, out_specs=out_specs, check_vma=False
    )
```

```python
import functools

import jax
import jax.numpy as jnp
from jax import lax
from jax.experimental import pallas as pl
from jax.experimental.pallas import tpu as pltpu
from jax.sharding import Mesh, PartitionSpec as P

support_radius = 0.12
stretch = 4.0 / support_radius
depth = 128
span = 256
whole = pl.BlockSpec(memory_space=pltpu.VMEM)
params = pltpu.CompilerParams(vmem_limit_bytes=16 * 1024 * 1024)


def pieces_of(values):
    high = values.astype(jnp.bfloat16).astype(jnp.float32)
    rest = values - high
    middle = rest.astype(jnp.bfloat16).astype(jnp.float32)
    low = (rest - middle).astype(jnp.bfloat16).astype(jnp.float32)
    return high, middle, low


def write_features(xyz_ref, rows, is_node):
    count = xyz_ref.shape[1]
    place = (xyz_ref[...] - 0.5) * stretch
    norm = (
        place[0:1] * place[0:1] + place[1:2] * place[1:2] + place[2:3] * place[2:3]
    )
    parts = pieces_of(place)
    norm_parts = pieces_of(norm)
    ones = jnp.ones((3, count), jnp.float32)
    rows[...] = jnp.zeros_like(rows)
    for i in range(3):
        for j in range(3):
            k = 3 * (3 * i + j)
            rows[k : k + 3, :] = parts[i] if is_node else -2.0 * parts[j]
    norm_at, ones_at = (27, 30) if is_node else (30, 27)
    rows[ones_at : ones_at + 3, :] = ones
    for i in range(3):
        rows[norm_at + i : norm_at + i + 1, :] = norm_parts[i]


def features_kernel(node_ref, ctrl_ref, node_out, ctrl_out, node_rows, ctrl_rows):
    write_features(node_ref, node_rows, True)
    write_features(ctrl_ref, ctrl_rows, False)
    ctrl_out[...] = ctrl_rows[...].astype(jnp.bfloat16)
    node_out[...] = node_rows[...].T.astype(jnp.bfloat16)


def features(node_xyz, ctrl_xyz):
    nodes, ctrls = node_xyz.shape[1], ctrl_xyz.shape[1]
    return pl.pallas_call(
        features_kernel,
        out_shape=[
            jax.ShapeDtypeStruct((nodes, depth), jnp.bfloat16),
            jax.ShapeDtypeStruct((depth, ctrls), jnp.bfloat16),
        ],
        scratch_shapes=[
            pltpu.VMEM((depth, nodes), jnp.float32),
            pltpu.VMEM((depth, ctrls), jnp.float32),
        ],
        cost_estimate=pl.CostEstimate(
            flops=nodes * 1000, bytes_accessed=nodes * 512, transcendentals=0
        ),
        in_specs=[whole] * 2,
        out_specs=[whole] * 2,
        compiler_params=params,
        name="features",
    )(node_xyz, ctrl_xyz)


def wendland(squared):
    squared = jnp.maximum(squared, 1e-30)
    r4 = squared * lax.rsqrt(squared)
    remain = jnp.maximum(4.0 - r4, 0.0)
    remain2 = remain * remain
    return (remain2 * remain2 * (r4 + 1.0)).astype(jnp.bfloat16)


def pull_kernel(tile, other, first, blocks, add_at, *refs):
    node_ref, ctrl_ref, sens_ref, out_ref = refs[0], refs[1], refs[2], refs[-1]
    nodes = node_ref.shape[0]
    core = lax.axis_index("core")
    x = lax.axis_index("x")
    half = (1 - core) if other else core
    for j in range(blocks):
        quarter = lax.rem(x + first + j, 4)
        from_column = pl.multiple_of((half * 4 + quarter) * span, span)
        weights = ctrl_ref[:, pl.ds(from_column, span)]

        def body(i, acc):
            at = pl.multiple_of(i * tile, tile)
            squared = jnp.dot(
                node_ref[pl.ds(at, tile), :],
                weights,
                preferred_element_type=jnp.float32,
            )
            return acc + jnp.dot(
                sens_ref[:, pl.ds(at, tile)],
                wendland(squared),
                preferred_element_type=jnp.float32,
            )

        acc = lax.fori_loop(
            0, nodes // tile, body, jnp.zeros((out_ref.shape[0], span), jnp.float32)
        )
        acc = acc * (1.0 / 256.0)
        if len(refs) == 5:
            acc = acc + refs[3][:, add_at * span : (add_at + 1) * span]
        out_ref[:, j * span : (j + 1) * span] = acc


def pull(
    other, first, blocks, node_feat, ctrl_feat, sens, add=None, add_at=0, tile=2048
):
    nodes = node_feat.shape[0]
    rows = sens.shape[0]
    args = [node_feat, ctrl_feat, sens] + ([] if add is None else [add])
    return pl.pallas_call(
        functools.partial(pull_kernel, tile, other, first, blocks, add_at),
        out_shape=jax.ShapeDtypeStruct((rows, blocks * span), jnp.float32),
        in_specs=[whole] * len(args),
        out_specs=whole,
        cost_estimate=pl.CostEstimate(
            flops=blocks * span * nodes * 400,
            bytes_accessed=nodes * 448,
            transcendentals=blocks * span * nodes,
        ),
        compiler_params=params,
        name="pull",
    )(*args)


def product_kernel(order, *refs):
    blocks, inverse_ref, out_ref = refs[:-2], refs[-2], refs[-1]
    core = lax.axis_index("core")
    x = lax.axis_index("x")
    total = None
    for half, joined in ((core, blocks[:-1]), (1 - core, blocks[-1:])):
        for i, by in enumerate(order):
            at = pl.multiple_of((half * 4 + lax.rem(x + 4 - by, 4)) * span, span)
            if len(joined) == 1:
                block = joined[0][:, i * span : (i + 1) * span]
            else:
                block = joined[i][...]
            term = jnp.dot(
                block,
                inverse_ref[pl.ds(at, span), :],
                preferred_element_type=jnp.float32,
            )
            total = term if total is None else total + term
    shares, rows, lanes = out_ref.shape
    width = lanes // 2
    for j in range(shares):
        share = total[:, j * width : (j + 1) * width]
        out_ref[j] = jnp.concatenate([share[:rows], share[rows:]], axis=1).astype(
            out_ref.dtype
        )


def product(order, blocks, inverse, shares):
    rows, width = blocks[0].shape[0], inverse.shape[1] // shares
    return pl.pallas_call(
        functools.partial(product_kernel, order),
        out_shape=jax.ShapeDtypeStruct((shares, rows // 2, 2 * width), jnp.bfloat16),
        in_specs=[whole] * (len(blocks) + 1),
        out_specs=whole,
        compiler_params=params,
        name="product",
    )(*blocks, inverse)


def finish_kernel(shares_ref, out_ref):
    total = shares_ref[0].astype(jnp.float32)
    for j in range(1, shares_ref.shape[0]):
        total = total + shares_ref[j].astype(jnp.float32)
    rows, lanes = total.shape
    turned = total.T
    out_ref[:, 0:rows] = turned[: lanes // 2]
    out_ref[:, rows:] = turned[lanes // 2 :]


def finish(shares):
    _, rows, lanes = shares.shape
    return pl.pallas_call(
        finish_kernel,
        out_shape=jax.ShapeDtypeStruct((lanes // 2, 2 * rows), jnp.float32),
        in_specs=[whole],
        out_specs=whole,
        compiler_params=params,
        name="finish",
    )(shares).T


def shifted(value, axis, by):
    size = lax.axis_size(axis)
    return lax.ppermute(value, axis, [(i, (i + by) % size) for i in range(size)])


def per_device(sensitivity, node_xyz, ctrl_xyz, inverse):
    node_feat, ctrl_feat = features(node_xyz, ctrl_xyz)
    pulled = functools.partial(
        pull, node_feat=node_feat, ctrl_feat=ctrl_feat, sens=sensitivity
    )
    sent_on = shifted(pulled(True, 1, 3), "core", 1)
    kept = shifted(pulled(True, 0, 1), "core", 1)
    order = (2, 1, 3)
    arrived = [
        shifted(pulled(False, by, 1, add=sent_on, add_at=by - 1), "x", by)
        for by in order
    ]
    summed = pulled(False, 0, 1, add=kept)
    for part in arrived:
        summed = summed + part

    low = summed.astype(jnp.bfloat16)
    for by in order:
        summed = summed + shifted(low, "zh", by).astype(jnp.float32)
    mine = summed.astype(jnp.bfloat16)

    along_x = [mine] + [shifted(mine, "x", by) for by in order]
    swapped = shifted(jnp.concatenate(along_x, axis=1), "core", 1)
    shares = product((0,) + order, along_x + [swapped], inverse, 8)
    arrived_shares = lax.all_to_all(
        shares, ("y", "zl"), split_axis=0, concat_axis=0, tiled=True
    )
    return finish(arrived_shares)


def solution(mesh):
    fine = Mesh(
        mesh.devices.reshape(4, 4, 2, 4, 2), ("zh", "x", "core", "y", "zl")
    )
    node, ctrl = ("zh", "x", "core"), ("y", "zl")
    in_specs = (P(None, node), P(None, node), P(None, ctrl), P(ctrl, node))
    out_specs = P(None, node + ctrl)
    return jax.shard_map(
        per_device, mesh=fine, in_specs=in_specs, out_specs=out_specs, check_vma=False
    )
```

```python
import functools

import jax
import jax.numpy as jnp
from jax import lax
from jax.experimental import pallas as pl
from jax.experimental.pallas import tpu as pltpu
from jax.sharding import Mesh, PartitionSpec as P


support_radius = 0.12
stretch = 4.0 / support_radius
depth = 128
span = 256
whole = pl.BlockSpec(memory_space=pltpu.VMEM)
params = pltpu.CompilerParams(vmem_limit_bytes=16 * 1024 * 1024)


def pieces_of(values):
    high = values.astype(jnp.bfloat16).astype(jnp.float32)
    rest = values - high
    middle = rest.astype(jnp.bfloat16).astype(jnp.float32)
    low = (rest - middle).astype(jnp.bfloat16).astype(jnp.float32)
    return high, middle, low


def write_features(xyz_ref, rows, is_node):
    count = xyz_ref.shape[1]
    place = (xyz_ref[...] - 0.5) * stretch
    norm = (
        place[0:1] * place[0:1] + place[1:2] * place[1:2] + place[2:3] * place[2:3]
    )
    parts = pieces_of(place)
    norm_parts = pieces_of(norm)
    ones = jnp.ones((3, count), jnp.float32)
    rows[...] = jnp.zeros_like(rows)
    for i in range(3):
        for j in range(3):
            k = 3 * (3 * i + j)
            rows[k : k + 3, :] = parts[i] if is_node else -2.0 * parts[j]
    norm_at, ones_at = (27, 30) if is_node else (30, 27)
    rows[ones_at : ones_at + 3, :] = ones
    for i in range(3):
        rows[norm_at + i : norm_at + i + 1, :] = norm_parts[i]


def wendland(squared):
    squared = jnp.maximum(squared, 1e-30)
    r4 = squared * lax.rsqrt(squared)
    remain = jnp.maximum(4.0 - r4, 0.0)
    remain2 = remain * remain
    return (remain2 * remain2 * (r4 + 1.0)).astype(jnp.bfloat16)


def pulled_block(node_ref, ctrl_ref, sens_ref, block):
    columns = pl.ds(pl.multiple_of(block * span, span), span)
    squared = jnp.dot(
        node_ref[...], ctrl_ref[:, columns], preferred_element_type=jnp.float32
    )
    total = jnp.dot(
        sens_ref[...], wendland(squared), preferred_element_type=jnp.float32
    )
    return total * (1.0 / 256.0)


def first_kernel(
    by, sens_in, node_in, ctrl_in, out_ref, node_ref, ctrl_ref, sens_ref, *scratch
):
    node_xyz, ctrl_xyz, node_rows, ctrl_rows, done = scratch
    copies = [
        pltpu.make_async_copy(source, target, done.at[i])
        for i, (source, target) in enumerate(
            ((node_in, node_xyz), (ctrl_in, ctrl_xyz), (sens_in, sens_ref))
        )
    ]
    for copy in copies:
        copy.start()
    copies[0].wait()
    write_features(node_xyz, node_rows, True)
    node_ref[...] = node_rows[...].T.astype(jnp.bfloat16)
    copies[1].wait()
    write_features(ctrl_xyz, ctrl_rows, False)
    ctrl_ref[...] = ctrl_rows[...].astype(jnp.bfloat16)
    copies[2].wait()
    block = (1 - lax.axis_index("core")) * 4 + lax.bitwise_xor(lax.axis_index("x"), by)
    out_ref[...] = pulled_block(node_ref, ctrl_ref, sens_ref, block)


def pull_cost(nodes, blocks):
    return pl.CostEstimate(
        flops=blocks * span * nodes * 400,
        bytes_accessed=nodes * 448,
        transcendentals=blocks * span * nodes,
    )


def first_pull(by, sens, node_xyz, ctrl_xyz):
    rows, nodes = sens.shape
    ctrls = ctrl_xyz.shape[1]
    return pl.pallas_call(
        functools.partial(first_kernel, by),
        out_shape=[
            jax.ShapeDtypeStruct((rows, span), jnp.float32),
            jax.ShapeDtypeStruct((nodes, depth), jnp.bfloat16),
            jax.ShapeDtypeStruct((depth, ctrls), jnp.bfloat16),
            jax.ShapeDtypeStruct(sens.shape, sens.dtype),
        ],
        in_specs=[pl.BlockSpec(memory_space=pltpu.HBM)] * 3,
        out_specs=[whole] * 4,
        scratch_shapes=[
            pltpu.VMEM(node_xyz.shape, jnp.float32),
            pltpu.VMEM(ctrl_xyz.shape, jnp.float32),
            pltpu.VMEM((depth, nodes), jnp.float32),
            pltpu.VMEM((depth, ctrls), jnp.float32),
            pltpu.SemaphoreType.DMA((3,)),
        ],
        cost_estimate=pull_cost(nodes, 2),
        compiler_params=params,
        name="first_pull",
    )(*(pltpu.with_memory_space_constraint(a, pltpu.HBM) for a in (sens, node_xyz, ctrl_xyz)))


def pull_kernel(other, steps, add_at, node_ref, ctrl_ref, sens_ref, *rest):
    out_ref = rest[-1]
    core = lax.axis_index("core")
    x = lax.axis_index("x")
    half = (1 - core) if other else core
    if len(steps) == 1:
        block = half * 4 + lax.bitwise_xor(x, steps[0])
        total = pulled_block(node_ref, ctrl_ref, sens_ref, block)
        if len(rest) == 2:
            total = total + rest[0][:, add_at * span : (add_at + 1) * span]
        out_ref[...] = total
        return

    def body(j, carry):
        block = half * 4 + lax.bitwise_xor(x, steps[0] + j * (steps[1] - steps[0]))
        columns = pl.ds(pl.multiple_of(j * span, span), span)
        out_ref[:, columns] = pulled_block(node_ref, ctrl_ref, sens_ref, block)
        return carry

    lax.fori_loop(0, len(steps), body, 0)


def pull(prepared, other, steps, add=None, add_at=0):
    rows, nodes = prepared[2].shape
    args = list(prepared) + ([] if add is None else [add])
    return pl.pallas_call(
        functools.partial(pull_kernel, other, steps, add_at),
        out_shape=jax.ShapeDtypeStruct((rows, len(steps) * span), jnp.float32),
        in_specs=[whole] * len(args),
        out_specs=whole,
        cost_estimate=pull_cost(nodes, len(steps)),
        compiler_params=params,
        name="pull",
    )(*args)


def product_kernel(order, *refs):
    blocks, inverse_ref, out_ref = refs[:-2], refs[-2], refs[-1]
    core = lax.axis_index("core")
    x = lax.axis_index("x")
    total = None
    for half, joined in ((core, blocks[:-1]), (1 - core, blocks[-1:])):
        for i, by in enumerate(order):
            at = pl.multiple_of((half * 4 + lax.bitwise_xor(x, by)) * span, span)
            if len(joined) == 1:
                block = joined[0][:, i * span : (i + 1) * span]
            else:
                block = joined[i][...]
            term = jnp.dot(
                block,
                inverse_ref[pl.ds(at, span), :],
                preferred_element_type=jnp.float32,
            )
            total = term if total is None else total + term
    shares, rows, lanes = out_ref.shape
    width = lanes // 2
    for j in range(shares):
        share = total[:, j * width : (j + 1) * width]
        out_ref[j] = jnp.concatenate([share[:rows], share[rows:]], axis=1).astype(
            out_ref.dtype
        )


def product(order, blocks, inverse, shares):
    rows, width = blocks[0].shape[0], inverse.shape[1] // shares
    return pl.pallas_call(
        functools.partial(product_kernel, order),
        out_shape=jax.ShapeDtypeStruct((shares, rows // 2, 2 * width), jnp.bfloat16),
        in_specs=[whole] * (len(blocks) + 1),
        out_specs=whole,
        compiler_params=params,
        name="product",
    )(*blocks, inverse)


def finish_kernel(shares_ref, out_ref):
    total = shares_ref[0].astype(jnp.float32)
    for j in range(1, shares_ref.shape[0]):
        total = total + shares_ref[j].astype(jnp.float32)
    rows, lanes = total.shape
    turned = total.T
    out_ref[:, 0:rows] = turned[: lanes // 2]
    out_ref[:, rows:] = turned[lanes // 2 :]


def finish(shares):
    _, rows, lanes = shares.shape
    return pl.pallas_call(
        finish_kernel,
        out_shape=jax.ShapeDtypeStruct((lanes // 2, 2 * rows), jnp.float32),
        in_specs=[whole],
        out_specs=whole,
        compiler_params=params,
        name="finish",
    )(shares).T


def swapped(value, axis, by):
    size = lax.axis_size(axis)
    return lax.ppermute(value, axis, [(i, i ^ by) for i in range(size)])


def per_device(sensitivity, node_xyz, ctrl_xyz, inverse):
    def pulled(*args):
        return pull(prepared, *args)

    first, *prepared = first_pull(2, sensitivity, node_xyz, ctrl_xyz)
    first = swapped(first, "core", 1)
    second = swapped(pulled(True, (1, 3)), "core", 1)
    parts = [
        swapped(pulled(False, (2,), first), "x", 2),
        swapped(pulled(False, (1,), second, 0), "x", 1),
        swapped(pulled(False, (3,), second, 1), "x", 3),
        swapped(pulled(True, (0,)), "core", 1),
    ]
    summed = pulled(False, (0,))
    for part in parts:
        summed = summed + part

    low = summed.astype(jnp.bfloat16)
    for by in (2, 1, 3):
        summed = summed + swapped(low, "zh", by).astype(jnp.float32)
    mine = summed.astype(jnp.bfloat16)

    order = (2, 1, 3)
    along_x = [mine] + [swapped(mine, "x", by) for by in order]
    across = swapped(jnp.concatenate(along_x, axis=1), "core", 1)
    shares = product((0,) + order, along_x + [across], inverse, 8)
    arrived_shares = lax.all_to_all(
        shares, ("y", "zl"), split_axis=0, concat_axis=0, tiled=True
    )
    return finish(arrived_shares)


def solution(mesh):
    fine = Mesh(
        mesh.devices.reshape(4, 4, 2, 4, 2), ("zh", "x", "core", "y", "zl")
    )
    node, ctrl = ("zh", "x", "core"), ("y", "zl")
    in_specs = (P(None, node), P(None, node), P(None, ctrl), P(ctrl, node))
    out_specs = P(None, node + ctrl)

    return jax.shard_map(
        per_device, mesh=fine, in_specs=in_specs, out_specs=out_specs, check_vma=False
    )
```

```python
import functools

import jax
import jax.numpy as jnp
from jax import lax
from jax.experimental import pallas as pl
from jax.experimental.pallas import tpu as pltpu
from jax.sharding import Mesh, PartitionSpec as P


support_radius = 0.12
stretch = 4.0 / support_radius
depth = 128
used = 40
span = 256
whole = pl.BlockSpec(memory_space=pltpu.VMEM)
params = pltpu.CompilerParams(vmem_limit_bytes=16 * 1024 * 1024)


def pieces_of(values):
    high = values.astype(jnp.bfloat16).astype(jnp.float32)
    rest = values - high
    middle = rest.astype(jnp.bfloat16).astype(jnp.float32)
    low = (rest - middle).astype(jnp.bfloat16).astype(jnp.float32)
    return high, middle, low


def write_features(xyz_ref, rows, is_node):
    count = xyz_ref.shape[1]
    place = (xyz_ref[...] - 0.5) * stretch
    norm = (
        place[0:1] * place[0:1] + place[1:2] * place[1:2] + place[2:3] * place[2:3]
    )
    parts = pieces_of(place)
    norm_parts = pieces_of(norm)
    ones = jnp.ones((3, count), jnp.float32)
    rows[...] = jnp.zeros_like(rows)
    for i in range(3):
        for j in range(3):
            k = 3 * (3 * i + j)
            rows[k : k + 3, :] = parts[i] if is_node else -2.0 * parts[j]
    norm_at, ones_at = (27, 30) if is_node else (30, 27)
    rows[ones_at : ones_at + 3, :] = ones
    for i in range(3):
        rows[norm_at + i : norm_at + i + 1, :] = norm_parts[i]


def wendland(squared):
    squared = jnp.maximum(squared, 1e-30)
    r4 = squared * lax.rsqrt(squared)
    remain = jnp.maximum(4.0 - r4, 0.0)
    remain2 = remain * remain
    return (remain2 * remain2 * (r4 + 1.0)).astype(jnp.bfloat16)


def pulled_block(node_ref, ctrl_ref, sens_ref, block):
    columns = pl.ds(pl.multiple_of(block * span, span), span)
    squared = jnp.dot(
        node_ref[...], ctrl_ref[:, columns], preferred_element_type=jnp.float32
    )
    total = jnp.dot(
        sens_ref[...], wendland(squared), preferred_element_type=jnp.float32
    )
    return total * (1.0 / 256.0)


def first_kernel(
    steps, sens_in, node_in, ctrl_in, out_ref, node_ref, ctrl_ref, sens_ref, *scratch
):
    node_xyz, ctrl_xyz, node_rows, ctrl_rows, done = scratch
    copies = [
        pltpu.make_async_copy(source, target, done.at[i])
        for i, (source, target) in enumerate(
            ((node_in, node_xyz), (ctrl_in, ctrl_xyz), (sens_in, sens_ref))
        )
    ]
    for copy in copies:
        copy.start()
    node_ref[...] = jnp.zeros_like(node_ref)
    ctrl_ref[...] = jnp.zeros_like(ctrl_ref)
    for copy in copies:
        copy.wait()
    write_features(node_xyz, node_rows, True)
    node_ref[:, 0:used] = node_rows[...].T.astype(jnp.bfloat16)
    write_features(ctrl_xyz, ctrl_rows, False)
    ctrl_ref[0:used, :] = ctrl_rows[...].astype(jnp.bfloat16)
    core = lax.axis_index("core")
    x = lax.axis_index("x")
    for j, step in enumerate(steps):
        block = (1 - core) * 4 + lax.bitwise_xor(x, step)
        out_ref[:, j * span : (j + 1) * span] = pulled_block(
            node_ref, ctrl_ref, sens_ref, block
        )


def pull_cost(nodes, blocks):
    return pl.CostEstimate(
        flops=blocks * span * nodes * 400,
        bytes_accessed=nodes * 448,
        transcendentals=blocks * span * nodes,
    )


def first_pull(steps, sens, node_xyz, ctrl_xyz):
    rows, nodes = sens.shape
    ctrls = ctrl_xyz.shape[1]
    return pl.pallas_call(
        functools.partial(first_kernel, steps),
        out_shape=[
            jax.ShapeDtypeStruct((rows, len(steps) * span), jnp.float32),
            jax.ShapeDtypeStruct((nodes, depth), jnp.bfloat16),
            jax.ShapeDtypeStruct((depth, ctrls), jnp.bfloat16),
            jax.ShapeDtypeStruct(sens.shape, sens.dtype),
        ],
        in_specs=[pl.BlockSpec(memory_space=pltpu.HBM)] * 3,
        out_specs=[whole] * 4,
        scratch_shapes=[
            pltpu.VMEM(node_xyz.shape, jnp.float32),
            pltpu.VMEM(ctrl_xyz.shape, jnp.float32),
            pltpu.VMEM((used, nodes), jnp.float32),
            pltpu.VMEM((used, ctrls), jnp.float32),
            pltpu.SemaphoreType.DMA((3,)),
        ],
        cost_estimate=pull_cost(nodes, len(steps)),
        compiler_params=params,
        name="first_pull",
    )(*(pltpu.with_memory_space_constraint(a, pltpu.HBM) for a in (sens, node_xyz, ctrl_xyz)))


def pull_kernel(other, step, add_at, node_ref, ctrl_ref, sens_ref, *rest):
    core = lax.axis_index("core")
    half = (1 - core) if other else core
    block = half * 4 + lax.bitwise_xor(lax.axis_index("x"), step)
    total = pulled_block(node_ref, ctrl_ref, sens_ref, block)
    if len(rest) == 2:
        total = total + rest[0][:, add_at * span : (add_at + 1) * span]
    rest[-1][...] = total


def pull(prepared, other, step, add=None, add_at=0):
    rows, nodes = prepared[2].shape
    args = list(prepared) + ([] if add is None else [add])
    return pl.pallas_call(
        functools.partial(pull_kernel, other, step, add_at),
        out_shape=jax.ShapeDtypeStruct((rows, span), jnp.float32),
        in_specs=[whole] * len(args),
        out_specs=whole,
        cost_estimate=pull_cost(nodes, 1),
        compiler_params=params,
        name="pull",
    )(*args)


def product_kernel(order, *refs):
    blocks, inverse_ref, out_ref = refs[:-2], refs[-2], refs[-1]
    core = lax.axis_index("core")
    x = lax.axis_index("x")
    total = None
    for half, joined in ((core, blocks[:-1]), (1 - core, blocks[-1:])):
        for i, by in enumerate(order):
            at = pl.multiple_of((half * 4 + lax.bitwise_xor(x, by)) * span, span)
            if len(joined) == 1:
                block = joined[0][:, i * span : (i + 1) * span]
            else:
                block = joined[i][...]
            term = jnp.dot(
                block,
                inverse_ref[pl.ds(at, span), :],
                preferred_element_type=jnp.float32,
            )
            total = term if total is None else total + term
    shares, rows, lanes = out_ref.shape
    width = lanes // 2
    for j in range(shares):
        share = total[:, j * width : (j + 1) * width]
        out_ref[j] = jnp.concatenate([share[:rows], share[rows:]], axis=1).astype(
            out_ref.dtype
        )


def product(order, blocks, inverse, shares):
    rows, width = blocks[0].shape[0], inverse.shape[1] // shares
    return pl.pallas_call(
        functools.partial(product_kernel, order),
        out_shape=jax.ShapeDtypeStruct((shares, rows // 2, 2 * width), jnp.bfloat16),
        in_specs=[whole] * (len(blocks) + 1),
        out_specs=whole,
        compiler_params=params,
        name="product",
    )(*blocks, inverse)


def finish_kernel(shares_ref, out_ref):
    total = shares_ref[0].astype(jnp.float32)
    for j in range(1, shares_ref.shape[0]):
        total = total + shares_ref[j].astype(jnp.float32)
    rows, lanes = total.shape
    turned = total.T
    out_ref[:, 0:rows] = turned[: lanes // 2]
    out_ref[:, rows:] = turned[lanes // 2 :]


def finish(shares):
    _, rows, lanes = shares.shape
    return pl.pallas_call(
        finish_kernel,
        out_shape=jax.ShapeDtypeStruct((lanes // 2, 2 * rows), jnp.float32),
        in_specs=[whole],
        out_specs=whole,
        compiler_params=params,
        name="finish",
    )(shares).T


def swapped(value, axis, by):
    size = lax.axis_size(axis)
    return lax.ppermute(value, axis, [(i, i ^ by) for i in range(size)])


def per_device(sensitivity, node_xyz, ctrl_xyz, inverse):
    def pulled(*args):
        return pull(prepared, *args)

    steps = (2, 1, 3)
    shared, *prepared = first_pull(steps, sensitivity, node_xyz, ctrl_xyz)
    shared = swapped(shared, "core", 1)
    far = pulled(False, 2) + shared[:, :span]
    parts = [
        swapped(far, "x", 2),
        swapped(pulled(False, 1, shared, 1), "x", 1),
        swapped(pulled(False, 3, shared, 2), "x", 3),
        swapped(pulled(True, 0), "core", 1),
    ]
    summed = pulled(False, 0)
    for part in parts:
        summed = summed + part

    low = summed.astype(jnp.bfloat16)
    for by in (2, 1, 3):
        summed = summed + swapped(low, "zh", by).astype(jnp.float32)
    mine = summed.astype(jnp.bfloat16)

    order = (2, 1, 3)
    along_x = [mine] + [swapped(mine, "x", by) for by in order]
    across = swapped(jnp.concatenate(along_x, axis=1), "core", 1)
    shares = product((0,) + order, along_x + [across], inverse, 8)
    arrived_shares = lax.all_to_all(
        shares, ("y", "zl"), split_axis=0, concat_axis=0, tiled=True
    )
    return finish(arrived_shares)


def solution(mesh):
    fine = Mesh(
        mesh.devices.reshape(4, 4, 2, 4, 2), ("zh", "x", "core", "y", "zl")
    )
    node, ctrl = ("zh", "x", "core"), ("y", "zl")
    in_specs = (P(None, node), P(None, node), P(None, ctrl), P(ctrl, node))
    out_specs = P(None, node + ctrl)

    return jax.shard_map(
        per_device, mesh=fine, in_specs=in_specs, out_specs=out_specs, check_vma=False
    )
```

```python
import functools

import jax
import jax.numpy as jnp
from jax import lax
from jax.experimental import pallas as pl
from jax.experimental.pallas import tpu as pltpu
from jax.sharding import Mesh, PartitionSpec as P


support_radius = 0.12
stretch = 4.0 / support_radius
depth = 128
used = 40
span = 256
whole = pl.BlockSpec(memory_space=pltpu.VMEM)
params = pltpu.CompilerParams(vmem_limit_bytes=16 * 1024 * 1024)


def pieces_of(values):
    high = values.astype(jnp.bfloat16).astype(jnp.float32)
    rest = values - high
    middle = rest.astype(jnp.bfloat16).astype(jnp.float32)
    low = (rest - middle).astype(jnp.bfloat16).astype(jnp.float32)
    return high, middle, low


def write_features(xyz_ref, rows, is_node):
    count = xyz_ref.shape[1]
    place = (xyz_ref[...] - 0.5) * stretch
    norm = (
        place[0:1] * place[0:1] + place[1:2] * place[1:2] + place[2:3] * place[2:3]
    )
    parts = pieces_of(place)
    norm_parts = pieces_of(norm)
    ones = jnp.ones((3, count), jnp.float32)
    rows[...] = jnp.zeros_like(rows)
    for i in range(3):
        for j in range(3):
            k = 3 * (3 * i + j)
            rows[k : k + 3, :] = parts[i] if is_node else -2.0 * parts[j]
    norm_at, ones_at = (27, 30) if is_node else (30, 27)
    rows[ones_at : ones_at + 3, :] = ones
    for i in range(3):
        rows[norm_at + i : norm_at + i + 1, :] = norm_parts[i]


def wendland(squared):
    squared = jnp.maximum(squared, 1e-30)
    r4 = squared * lax.rsqrt(squared)
    remain = jnp.maximum(4.0 - r4, 0.0)
    remain2 = remain * remain
    return (remain2 * remain2 * (r4 + 1.0)).astype(jnp.bfloat16)


def pulled_block(node_ref, ctrl_ref, sens_ref, block):
    columns = pl.ds(pl.multiple_of(block * span, span), span)
    squared = jnp.dot(
        node_ref[...], ctrl_ref[:, columns], preferred_element_type=jnp.float32
    )
    total = jnp.dot(
        sens_ref[...], wendland(squared), preferred_element_type=jnp.float32
    )
    return total * (1.0 / 256.0)


def block_of(step):
    return lax.axis_index("core") * 4 + lax.bitwise_xor(lax.axis_index("x"), step)


def first_kernel(
    step, sens_in, node_in, ctrl_in, out_ref, node_ref, sens_ref, ctrl_ref, *scratch
):
    node_xyz, ctrl_xyz, node_rows, ctrl_rows, done = scratch
    copies = [
        pltpu.make_async_copy(source, target, done.at[i])
        for i, (source, target) in enumerate(
            ((node_in, node_xyz), (ctrl_in, ctrl_xyz), (sens_in, sens_ref))
        )
    ]
    for copy in copies:
        copy.start()
    node_ref[...] = jnp.zeros_like(node_ref)
    ctrl_ref[...] = jnp.zeros_like(ctrl_ref)
    for copy in copies:
        copy.wait()
    write_features(node_xyz, node_rows, True)
    node_ref[:, 0:used] = node_rows[...].T.astype(jnp.bfloat16)
    write_features(ctrl_xyz, ctrl_rows, False)
    ctrl_ref[0:used, :] = ctrl_rows[...].astype(jnp.bfloat16)
    out_ref[...] = pulled_block(node_ref, ctrl_ref, sens_ref, block_of(step))


def pull_cost(nodes, blocks):
    return pl.CostEstimate(
        flops=blocks * span * nodes * 400,
        bytes_accessed=nodes * 448,
        transcendentals=blocks * span * nodes,
    )


def first_pull(step, sens, node_xyz, ctrl_xyz):
    rows, nodes = sens.shape
    ctrls = ctrl_xyz.shape[1]
    return pl.pallas_call(
        functools.partial(first_kernel, step),
        out_shape=[
            jax.ShapeDtypeStruct((rows, span), jnp.float32),
            jax.ShapeDtypeStruct((nodes, depth), jnp.bfloat16),
            jax.ShapeDtypeStruct(sens.shape, sens.dtype),
            jax.ShapeDtypeStruct((depth, ctrls), jnp.bfloat16),
        ],
        in_specs=[pl.BlockSpec(memory_space=pltpu.HBM)] * 3,
        out_specs=[whole] * 4,
        scratch_shapes=[
            pltpu.VMEM(node_xyz.shape, jnp.float32),
            pltpu.VMEM(ctrl_xyz.shape, jnp.float32),
            pltpu.VMEM((used, nodes), jnp.float32),
            pltpu.VMEM((used, ctrls), jnp.float32),
            pltpu.SemaphoreType.DMA((3,)),
        ],
        cost_estimate=pull_cost(nodes, 1),
        compiler_params=params,
        name="first_pull",
    )(*(pltpu.with_memory_space_constraint(a, pltpu.HBM) for a in (sens, node_xyz, ctrl_xyz)))


def second_kernel(
    step, part_ref, node_xyz, sens_ref, ctrl_ref, out_ref, node_ref, node_rows
):
    node_ref[...] = jnp.zeros_like(node_ref)
    write_features(node_xyz, node_rows, True)
    node_ref[:, 0:used] = node_rows[...].T.astype(jnp.bfloat16)
    total = pulled_block(node_ref, ctrl_ref, sens_ref, block_of(step))
    out_ref[...] = total + part_ref[...]


def second_pull(step, part, node_xyz, sens, ctrl_feat):
    rows, nodes = sens.shape
    return pl.pallas_call(
        functools.partial(second_kernel, step),
        out_shape=[
            jax.ShapeDtypeStruct((rows, span), jnp.float32),
            jax.ShapeDtypeStruct((nodes, depth), jnp.bfloat16),
        ],
        in_specs=[whole] * 4,
        out_specs=[whole] * 2,
        scratch_shapes=[pltpu.VMEM((used, nodes), jnp.float32)],
        cost_estimate=pull_cost(nodes, 1),
        compiler_params=params,
        name="second_pull",
    )(part, node_xyz, sens, ctrl_feat)


def pull_kernel(step, node_a, sens_a, node_b, sens_b, ctrl_ref, out_ref):
    block = block_of(step)
    total = pulled_block(node_a, ctrl_ref, sens_a, block)
    out_ref[...] = total + pulled_block(node_b, ctrl_ref, sens_b, block)


def pull(step, *prepared):
    rows, nodes = prepared[1].shape
    return pl.pallas_call(
        functools.partial(pull_kernel, step),
        out_shape=jax.ShapeDtypeStruct((rows, span), jnp.float32),
        in_specs=[whole] * len(prepared),
        out_specs=whole,
        cost_estimate=pull_cost(nodes, 2),
        compiler_params=params,
        name="pull",
    )(*prepared)


def product_kernel(order, *refs):
    blocks, inverse_ref, out_ref = refs[:-2], refs[-2], refs[-1]
    core = lax.axis_index("core")
    x = lax.axis_index("x")
    total = None
    for half, joined in ((core, blocks[:-1]), (1 - core, blocks[-1:])):
        for i, by in enumerate(order):
            at = pl.multiple_of((half * 4 + lax.bitwise_xor(x, by)) * span, span)
            if len(joined) == 1:
                block = joined[0][:, i * span : (i + 1) * span]
            else:
                block = joined[i][...]
            term = jnp.dot(
                block,
                inverse_ref[pl.ds(at, span), :],
                preferred_element_type=jnp.float32,
            )
            total = term if total is None else total + term
    shares, rows, lanes = out_ref.shape
    width = lanes // 2
    for j in range(shares):
        share = total[:, j * width : (j + 1) * width]
        out_ref[j] = jnp.concatenate([share[:rows], share[rows:]], axis=1).astype(
            out_ref.dtype
        )


def product(order, blocks, inverse, shares):
    rows, width = blocks[0].shape[0], inverse.shape[1] // shares
    return pl.pallas_call(
        functools.partial(product_kernel, order),
        out_shape=jax.ShapeDtypeStruct((shares, rows // 2, 2 * width), jnp.bfloat16),
        in_specs=[whole] * (len(blocks) + 1),
        out_specs=whole,
        compiler_params=params,
        name="product",
    )(*blocks, inverse)


def finish_kernel(shares_ref, out_ref):
    total = shares_ref[0].astype(jnp.float32)
    for j in range(1, shares_ref.shape[0]):
        total = total + shares_ref[j].astype(jnp.float32)
    rows, lanes = total.shape
    turned = total.T
    out_ref[:, 0:rows] = turned[: lanes // 2]
    out_ref[:, rows:] = turned[lanes // 2 :]


def finish(shares):
    _, rows, lanes = shares.shape
    return pl.pallas_call(
        finish_kernel,
        out_shape=jax.ShapeDtypeStruct((lanes // 2, 2 * rows), jnp.float32),
        in_specs=[whole],
        out_specs=whole,
        compiler_params=params,
        name="finish",
    )(shares).T


def swapped(value, axis, by):
    size = lax.axis_size(axis)
    return lax.ppermute(value, axis, [(i, i ^ by) for i in range(size)])


def per_device(sensitivity, node_xyz, ctrl_xyz, inverse):
    other_sens = swapped(sensitivity, "core", 1)
    other_xyz = swapped(node_xyz, "core", 1)
    far, node_feat, sens, ctrl_feat = first_pull(
        2, sensitivity, node_xyz, ctrl_xyz
    )
    far, other_feat = second_pull(2, far, other_xyz, other_sens, ctrl_feat)
    prepared = (node_feat, sens, other_feat, other_sens, ctrl_feat)
    parts = [swapped(far, "x", 2)]
    for step in (1, 3):
        block = pull(step, *prepared)
        parts.append(swapped(block, "x", step))
    summed = pull(0, *prepared)
    for part in parts:
        summed = summed + part

    low = summed.astype(jnp.bfloat16)
    for by in (2, 1, 3):
        summed = summed + swapped(low, "zh", by).astype(jnp.float32)
    mine = summed.astype(jnp.bfloat16)

    order = (2, 1, 3)
    along_x = [mine] + [swapped(mine, "x", by) for by in order]
    across = swapped(jnp.concatenate(along_x, axis=1), "core", 1)
    shares = product((0,) + order, along_x + [across], inverse, 8)
    arrived_shares = lax.all_to_all(
        shares, ("y", "zl"), split_axis=0, concat_axis=0, tiled=True
    )
    return finish(arrived_shares)


def solution(mesh):
    fine = Mesh(
        mesh.devices.reshape(4, 4, 2, 4, 2), ("zh", "x", "core", "y", "zl")
    )
    node, ctrl = ("zh", "x", "core"), ("y", "zl")
    in_specs = (P(None, node), P(None, node), P(None, ctrl), P(ctrl, node))
    out_specs = P(None, node + ctrl)

    return jax.shard_map(
        per_device, mesh=fine, in_specs=in_specs, out_specs=out_specs, check_vma=False
    )
```

```python
import functools

import jax
import jax.numpy as jnp
from jax import lax
from jax.experimental import pallas as pl
from jax.experimental.pallas import tpu as pltpu
from jax.sharding import Mesh, PartitionSpec as P


support_radius = 0.12
stretch = 4.0 / support_radius
depth = 128
used = 40
span = 256
whole = pl.BlockSpec(memory_space=pltpu.VMEM)
params = pltpu.CompilerParams(vmem_limit_bytes=16 * 1024 * 1024)


def pieces_of(values):
    high = values.astype(jnp.bfloat16).astype(jnp.float32)
    rest = values - high
    middle = rest.astype(jnp.bfloat16).astype(jnp.float32)
    low = (rest - middle).astype(jnp.bfloat16).astype(jnp.float32)
    return high, middle, low


def write_features(xyz_ref, rows, is_node):
    count = xyz_ref.shape[1]
    place = (xyz_ref[...] - 0.5) * stretch
    norm = (
        place[0:1] * place[0:1] + place[1:2] * place[1:2] + place[2:3] * place[2:3]
    )
    parts = pieces_of(place)
    norm_parts = pieces_of(norm)
    ones = jnp.ones((3, count), jnp.float32)
    rows[...] = jnp.zeros_like(rows)
    for i in range(3):
        for j in range(3):
            k = 3 * (3 * i + j)
            rows[k : k + 3, :] = parts[i] if is_node else -2.0 * parts[j]
    norm_at, ones_at = (27, 30) if is_node else (30, 27)
    rows[ones_at : ones_at + 3, :] = ones
    for i in range(3):
        rows[norm_at + i : norm_at + i + 1, :] = norm_parts[i]


def wendland(squared):
    squared = jnp.maximum(squared, 1e-30)
    r4 = squared * lax.rsqrt(squared)
    remain = jnp.maximum(4.0 - r4, 0.0)
    remain2 = remain * remain
    return (remain2 * remain2 * (r4 + 1.0)).astype(jnp.bfloat16)


def pulled_block(node_ref, ctrl_ref, sens_ref, block):
    columns = pl.ds(pl.multiple_of(block * span, span), span)
    squared = jnp.dot(
        node_ref[...], ctrl_ref[:, columns], preferred_element_type=jnp.float32
    )
    total = jnp.dot(
        sens_ref[...], wendland(squared), preferred_element_type=jnp.float32
    )
    return total * (1.0 / 256.0)


def block_of(step):
    return lax.axis_index("core") * 4 + lax.bitwise_xor(lax.axis_index("x"), step)


def first_kernel(
    step, sens_in, node_in, ctrl_in, out_ref, node_ref, sens_ref, ctrl_ref, *scratch
):
    node_xyz, ctrl_xyz, node_rows, ctrl_rows, done = scratch
    copies = [
        pltpu.make_async_copy(source, target, done.at[i])
        for i, (source, target) in enumerate(
            ((node_in, node_xyz), (ctrl_in, ctrl_xyz), (sens_in, sens_ref))
        )
    ]
    for copy in copies:
        copy.start()
    node_ref[...] = jnp.zeros_like(node_ref)
    ctrl_ref[...] = jnp.zeros_like(ctrl_ref)
    copies[0].wait()
    write_features(node_xyz, node_rows, True)
    node_ref[:, 0:used] = node_rows[...].T.astype(jnp.bfloat16)
    copies[1].wait()
    write_features(ctrl_xyz, ctrl_rows, False)
    ctrl_ref[0:used, :] = ctrl_rows[...].astype(jnp.bfloat16)
    copies[2].wait()
    out_ref[...] = pulled_block(node_ref, ctrl_ref, sens_ref, block_of(step))


def pull_cost(nodes, blocks):
    return pl.CostEstimate(
        flops=blocks * span * nodes * 400,
        bytes_accessed=nodes * 448,
        transcendentals=blocks * span * nodes,
    )


def first_pull(step, sens, node_xyz, ctrl_xyz):
    rows, nodes = sens.shape
    ctrls = ctrl_xyz.shape[1]
    return pl.pallas_call(
        functools.partial(first_kernel, step),
        out_shape=[
            jax.ShapeDtypeStruct((rows, span), jnp.float32),
            jax.ShapeDtypeStruct((nodes, depth), jnp.bfloat16),
            jax.ShapeDtypeStruct(sens.shape, sens.dtype),
            jax.ShapeDtypeStruct((depth, ctrls), jnp.bfloat16),
        ],
        in_specs=[pl.BlockSpec(memory_space=pltpu.HBM)] * 3,
        out_specs=[whole] * 4,
        scratch_shapes=[
            pltpu.VMEM(node_xyz.shape, jnp.float32),
            pltpu.VMEM(ctrl_xyz.shape, jnp.float32),
            pltpu.VMEM((used, nodes), jnp.float32),
            pltpu.VMEM((used, ctrls), jnp.float32),
            pltpu.SemaphoreType.DMA((3,)),
        ],
        cost_estimate=pull_cost(nodes, 1),
        compiler_params=params,
        name="first_pull",
    )(*(pltpu.with_memory_space_constraint(a, pltpu.HBM) for a in (sens, node_xyz, ctrl_xyz)))


def second_kernel(
    step, part_ref, node_xyz, sens_ref, ctrl_ref, out_ref, node_ref, node_rows
):
    node_ref[...] = jnp.zeros_like(node_ref)
    write_features(node_xyz, node_rows, True)
    node_ref[:, 0:used] = node_rows[...].T.astype(jnp.bfloat16)
    total = pulled_block(node_ref, ctrl_ref, sens_ref, block_of(step))
    out_ref[...] = total + part_ref[...]


def second_pull(step, part, node_xyz, sens, ctrl_feat):
    rows, nodes = sens.shape
    return pl.pallas_call(
        functools.partial(second_kernel, step),
        out_shape=[
            jax.ShapeDtypeStruct((rows, span), jnp.float32),
            jax.ShapeDtypeStruct((nodes, depth), jnp.bfloat16),
        ],
        in_specs=[whole] * 4,
        out_specs=[whole] * 2,
        scratch_shapes=[pltpu.VMEM((used, nodes), jnp.float32)],
        cost_estimate=pull_cost(nodes, 1),
        compiler_params=params,
        name="second_pull",
    )(part, node_xyz, sens, ctrl_feat)


def pull_kernel(step, node_a, sens_a, node_b, sens_b, ctrl_ref, out_ref):
    block = block_of(step)
    total = pulled_block(node_a, ctrl_ref, sens_a, block)
    out_ref[...] = total + pulled_block(node_b, ctrl_ref, sens_b, block)


def pull(step, *prepared):
    rows, nodes = prepared[1].shape
    return pl.pallas_call(
        functools.partial(pull_kernel, step),
        out_shape=jax.ShapeDtypeStruct((rows, span), jnp.float32),
        in_specs=[whole] * len(prepared),
        out_specs=whole,
        cost_estimate=pull_cost(nodes, 2),
        compiler_params=params,
        name="pull",
    )(*prepared)


def product_kernel(order, *refs):
    blocks, inverse_ref, out_ref = refs[:-2], refs[-2], refs[-1]
    core = lax.axis_index("core")
    x = lax.axis_index("x")
    total = None
    for half, joined in ((core, blocks[:-1]), (1 - core, blocks[-1:])):
        for i, by in enumerate(order):
            at = pl.multiple_of((half * 4 + lax.bitwise_xor(x, by)) * span, span)
            if len(joined) == 1:
                block = joined[0][:, i * span : (i + 1) * span]
            else:
                block = joined[i][...]
            term = jnp.dot(
                block,
                inverse_ref[pl.ds(at, span), :],
                preferred_element_type=jnp.float32,
            )
            total = term if total is None else total + term
    shares, rows, lanes = out_ref.shape
    width = lanes // 2
    for j in range(shares):
        share = total[:, j * width : (j + 1) * width]
        out_ref[j] = jnp.concatenate([share[:rows], share[rows:]], axis=1).astype(
            out_ref.dtype
        )


def product(order, blocks, inverse, shares):
    rows, width = blocks[0].shape[0], inverse.shape[1] // shares
    return pl.pallas_call(
        functools.partial(product_kernel, order),
        out_shape=jax.ShapeDtypeStruct((shares, rows // 2, 2 * width), jnp.bfloat16),
        in_specs=[whole] * (len(blocks) + 1),
        out_specs=whole,
        compiler_params=params,
        name="product",
    )(*blocks, inverse)


def finish_kernel(shares_ref, out_ref):
    total = shares_ref[0].astype(jnp.float32)
    for j in range(1, shares_ref.shape[0]):
        total = total + shares_ref[j].astype(jnp.float32)
    rows, lanes = total.shape
    turned = total.T
    out_ref[:, 0:rows] = turned[: lanes // 2]
    out_ref[:, rows:] = turned[lanes // 2 :]


def finish(shares):
    _, rows, lanes = shares.shape
    return pl.pallas_call(
        finish_kernel,
        out_shape=jax.ShapeDtypeStruct((lanes // 2, 2 * rows), jnp.float32),
        in_specs=[whole],
        out_specs=whole,
        compiler_params=params,
        name="finish",
    )(shares).T


def swapped(value, axis, by):
    size = lax.axis_size(axis)
    return lax.ppermute(value, axis, [(i, i ^ by) for i in range(size)])


def per_device(sensitivity, node_xyz, ctrl_xyz, inverse):
    other_sens = swapped(sensitivity, "core", 1)
    other_xyz = swapped(node_xyz, "core", 1)
    near, node_feat, sens, ctrl_feat = first_pull(1, sensitivity, node_xyz, ctrl_xyz)
    near, other_feat = second_pull(1, near, other_xyz, other_sens, ctrl_feat)
    prepared = (node_feat, sens, other_feat, other_sens, ctrl_feat)

    far = pull(2, *prepared)
    two = jnp.concatenate([near, far], axis=1).astype(jnp.bfloat16)
    two = swapped(two, "x", 1).astype(jnp.float32)
    right = pull(3, *prepared)
    right = swapped(right + two[:, span:], "x", 3)
    summed = pull(0, *prepared)
    summed = summed + two[:, :span] + right

    low = summed.astype(jnp.bfloat16)
    for by in (2, 1, 3):
        summed = summed + swapped(low, "zh", by).astype(jnp.float32)
    mine = summed.astype(jnp.bfloat16)

    order = (2, 1, 3)
    along_x = [mine] + [swapped(mine, "x", by) for by in order]
    across = swapped(jnp.concatenate(along_x, axis=1), "core", 1)
    shares = product((0,) + order, along_x + [across], inverse, 8)
    arrived_shares = lax.all_to_all(
        shares, ("y", "zl"), split_axis=0, concat_axis=0, tiled=True
    )
    return finish(arrived_shares)


def solution(mesh):
    fine = Mesh(
        mesh.devices.reshape(4, 4, 2, 4, 2), ("zh", "x", "core", "y", "zl")
    )
    node, ctrl = ("zh", "x", "core"), ("y", "zl")
    in_specs = (P(None, node), P(None, node), P(None, ctrl), P(ctrl, node))
    out_specs = P(None, node + ctrl)

    return jax.shard_map(
        per_device, mesh=fine, in_specs=in_specs, out_specs=out_specs, check_vma=False
    )
```

```python
import functools

import jax
import jax.numpy as jnp
from jax import lax
from jax.experimental import pallas as pl
from jax.experimental.pallas import tpu as pltpu
from jax.sharding import Mesh, PartitionSpec as P


support_radius = 0.12
stretch = 4.0 / support_radius
depth = 128
used = 40
span = 256
whole = pl.BlockSpec(memory_space=pltpu.VMEM)
params = pltpu.CompilerParams(vmem_limit_bytes=20 * 1024 * 1024)


def pieces_of(values):
    high = values.astype(jnp.bfloat16).astype(jnp.float32)
    rest = values - high
    middle = rest.astype(jnp.bfloat16).astype(jnp.float32)
    low = (rest - middle).astype(jnp.bfloat16).astype(jnp.float32)
    return high, middle, low


def write_features(xyz_ref, rows, is_node):
    count = xyz_ref.shape[1]
    place = (xyz_ref[...] - 0.5) * stretch
    norm = (
        place[0:1] * place[0:1] + place[1:2] * place[1:2] + place[2:3] * place[2:3]
    )
    parts = pieces_of(place)
    norm_parts = pieces_of(norm)
    ones = jnp.ones((3, count), jnp.float32)
    rows[...] = jnp.zeros_like(rows)
    for i in range(3):
        for j in range(3):
            k = 3 * (3 * i + j)
            rows[k : k + 3, :] = parts[i] if is_node else -2.0 * parts[j]
    norm_at, ones_at = (27, 30) if is_node else (30, 27)
    rows[ones_at : ones_at + 3, :] = ones
    for i in range(3):
        rows[norm_at + i : norm_at + i + 1, :] = norm_parts[i]


def wendland(squared):
    r4 = squared * lax.rsqrt(squared)
    remain = jnp.maximum(4.0 - r4, 0.0)
    remain2 = remain * remain
    return (remain2 * remain2 * (r4 + 1.0)).astype(jnp.bfloat16)


tile = 512


def block_scratch(nodes):
    return [
        pltpu.VMEM((nodes, span), jnp.float32),
        pltpu.VMEM((nodes, span), jnp.bfloat16),
    ]


def pulled_block(node_ref, ctrl_ref, sens_ref, block, squares, weights):
    columns = pl.ds(pl.multiple_of(block * span, span), span)
    tiles = node_ref.shape[0] // tile

    def square(i):
        at = slice(i * tile, (i + 1) * tile)
        product = jnp.dot(
            node_ref[at, :], ctrl_ref[:, columns], preferred_element_type=jnp.float32
        )
        squares[at, :] = jnp.maximum(product, 1e-30)

    def gather(i):
        at = slice(i * tile, (i + 1) * tile)
        return jnp.dot(
            sens_ref[:, at], weights[at, :], preferred_element_type=jnp.float32
        )

    total = None
    square(0)
    for i in range(tiles):
        if i + 1 < tiles:
            square(i + 1)
        at = slice(i * tile, (i + 1) * tile)
        weights[at, :] = wendland(squares[at, :])
        if i > 0:
            term = gather(i - 1)
            total = term if total is None else total + term
    last = gather(tiles - 1)
    total = last if total is None else total + last
    return total * (1.0 / 256.0)


def block_of(step):
    return lax.axis_index("core") * 4 + lax.bitwise_xor(lax.axis_index("x"), step)


def first_kernel(
    step, sens_in, node_in, ctrl_in, out_ref, node_ref, sens_ref, ctrl_ref, *scratch
):
    node_xyz, ctrl_xyz, node_rows, ctrl_rows, done, squares, weights = scratch
    copies = [
        pltpu.make_async_copy(source, target, done.at[i])
        for i, (source, target) in enumerate(
            ((node_in, node_xyz), (ctrl_in, ctrl_xyz), (sens_in, sens_ref))
        )
    ]
    for copy in copies:
        copy.start()
    node_ref[...] = jnp.zeros_like(node_ref)
    ctrl_ref[...] = jnp.zeros_like(ctrl_ref)
    copies[0].wait()
    write_features(node_xyz, node_rows, True)
    node_ref[:, 0:used] = node_rows[...].T.astype(jnp.bfloat16)
    copies[1].wait()
    write_features(ctrl_xyz, ctrl_rows, False)
    ctrl_ref[0:used, :] = ctrl_rows[...].astype(jnp.bfloat16)
    copies[2].wait()
    out_ref[...] = pulled_block(
        node_ref, ctrl_ref, sens_ref, block_of(step), squares, weights
    )


def pull_cost(nodes, blocks):
    return pl.CostEstimate(
        flops=blocks * span * nodes * 400,
        bytes_accessed=nodes * 448,
        transcendentals=blocks * span * nodes,
    )


def first_pull(step, sens, node_xyz, ctrl_xyz):
    rows, nodes = sens.shape
    ctrls = ctrl_xyz.shape[1]
    return pl.pallas_call(
        functools.partial(first_kernel, step),
        out_shape=[
            jax.ShapeDtypeStruct((rows, span), jnp.float32),
            jax.ShapeDtypeStruct((nodes, depth), jnp.bfloat16),
            jax.ShapeDtypeStruct(sens.shape, sens.dtype),
            jax.ShapeDtypeStruct((depth, ctrls), jnp.bfloat16),
        ],
        in_specs=[pl.BlockSpec(memory_space=pltpu.HBM)] * 3,
        out_specs=[whole] * 4,
        scratch_shapes=[
            pltpu.VMEM(node_xyz.shape, jnp.float32),
            pltpu.VMEM(ctrl_xyz.shape, jnp.float32),
            pltpu.VMEM((used, nodes), jnp.float32),
            pltpu.VMEM((used, ctrls), jnp.float32),
            pltpu.SemaphoreType.DMA((3,)),
        ]
        + block_scratch(nodes),
        cost_estimate=pull_cost(nodes, 1),
        compiler_params=params,
        name="first_pull",
    )(*(pltpu.with_memory_space_constraint(a, pltpu.HBM) for a in (sens, node_xyz, ctrl_xyz)))


def second_kernel(
    step, part_ref, node_xyz, sens_ref, ctrl_ref, out_ref, node_ref, node_rows, *scratch
):
    node_ref[...] = jnp.zeros_like(node_ref)
    write_features(node_xyz, node_rows, True)
    node_ref[:, 0:used] = node_rows[...].T.astype(jnp.bfloat16)
    total = pulled_block(node_ref, ctrl_ref, sens_ref, block_of(step), *scratch)
    out_ref[...] = total + part_ref[...]


def second_pull(step, part, node_xyz, sens, ctrl_feat):
    rows, nodes = sens.shape
    return pl.pallas_call(
        functools.partial(second_kernel, step),
        out_shape=[
            jax.ShapeDtypeStruct((rows, span), jnp.float32),
            jax.ShapeDtypeStruct((nodes, depth), jnp.bfloat16),
        ],
        in_specs=[whole] * 4,
        out_specs=[whole] * 2,
        scratch_shapes=[pltpu.VMEM((used, nodes), jnp.float32)] + block_scratch(nodes),
        cost_estimate=pull_cost(nodes, 1),
        compiler_params=params,
        name="second_pull",
    )(part, node_xyz, sens, ctrl_feat)


def pull_kernel(step, node_a, sens_a, node_b, sens_b, ctrl_ref, out_ref, *scratch):
    block = block_of(step)
    total = pulled_block(node_a, ctrl_ref, sens_a, block, *scratch[:2])
    out_ref[...] = total + pulled_block(node_b, ctrl_ref, sens_b, block, *scratch[2:])


def pull(step, *prepared):
    rows, nodes = prepared[1].shape
    return pl.pallas_call(
        functools.partial(pull_kernel, step),
        out_shape=jax.ShapeDtypeStruct((rows, span), jnp.float32),
        in_specs=[whole] * len(prepared),
        out_specs=whole,
        scratch_shapes=block_scratch(nodes) * 2,
        cost_estimate=pull_cost(nodes, 2),
        compiler_params=params,
        name="pull",
    )(*prepared)


def product_kernel(order, *refs):
    blocks, inverse_ref, out_ref = refs[:-2], refs[-2], refs[-1]
    core = lax.axis_index("core")
    x = lax.axis_index("x")
    total = None
    for half, joined in ((core, blocks[:-1]), (1 - core, blocks[-1:])):
        for i, by in enumerate(order):
            at = pl.multiple_of((half * 4 + lax.bitwise_xor(x, by)) * span, span)
            if len(joined) == 1:
                block = joined[0][:, i * span : (i + 1) * span]
            else:
                block = joined[i][...]
            term = jnp.dot(
                block,
                inverse_ref[pl.ds(at, span), :],
                preferred_element_type=jnp.float32,
            )
            total = term if total is None else total + term
    shares, rows, lanes = out_ref.shape
    width = lanes // 2
    for j in range(shares):
        share = total[:, j * width : (j + 1) * width]
        out_ref[j] = jnp.concatenate([share[:rows], share[rows:]], axis=1).astype(
            out_ref.dtype
        )


def product(order, blocks, inverse, shares):
    rows, width = blocks[0].shape[0], inverse.shape[1] // shares
    return pl.pallas_call(
        functools.partial(product_kernel, order),
        out_shape=jax.ShapeDtypeStruct((shares, rows // 2, 2 * width), jnp.bfloat16),
        in_specs=[whole] * (len(blocks) + 1),
        out_specs=whole,
        compiler_params=params,
        name="product",
    )(*blocks, inverse)


def finish_kernel(shares_ref, out_ref):
    total = shares_ref[0].astype(jnp.float32)
    for j in range(1, shares_ref.shape[0]):
        total = total + shares_ref[j].astype(jnp.float32)
    rows, lanes = total.shape
    turned = total.T
    out_ref[:, 0:rows] = turned[: lanes // 2]
    out_ref[:, rows:] = turned[lanes // 2 :]


def finish(shares):
    _, rows, lanes = shares.shape
    return pl.pallas_call(
        finish_kernel,
        out_shape=jax.ShapeDtypeStruct((lanes // 2, 2 * rows), jnp.float32),
        in_specs=[whole],
        out_specs=whole,
        compiler_params=params,
        name="finish",
    )(shares).T


def swapped(value, axis, by):
    size = lax.axis_size(axis)
    return lax.ppermute(value, axis, [(i, i ^ by) for i in range(size)])


def per_device(sensitivity, node_xyz, ctrl_xyz, inverse):
    other_sens = swapped(sensitivity, "core", 1)
    other_xyz = swapped(node_xyz, "core", 1)
    near, node_feat, sens, ctrl_feat = first_pull(1, sensitivity, node_xyz, ctrl_xyz)
    near, other_feat = second_pull(1, near, other_xyz, other_sens, ctrl_feat)
    prepared = (node_feat, sens, other_feat, other_sens, ctrl_feat)

    far = pull(2, *prepared)
    two = jnp.concatenate([near, far], axis=1).astype(jnp.bfloat16)
    two = swapped(two, "x", 1).astype(jnp.float32)
    right = pull(3, *prepared)
    right = (right + two[:, span:]).astype(jnp.bfloat16)
    right = swapped(right, "x", 3).astype(jnp.float32)
    summed = pull(0, *prepared)
    summed = summed + two[:, :span] + right

    low = summed.astype(jnp.bfloat16)
    for by in (2, 1, 3):
        summed = summed + swapped(low, "zh", by).astype(jnp.float32)
    mine = summed.astype(jnp.bfloat16)

    order = (2, 1, 3)
    along_x = [mine] + [swapped(mine, "x", by) for by in order]
    across = swapped(jnp.concatenate(along_x, axis=1), "core", 1)
    shares = product((0,) + order, along_x + [across], inverse, 8)
    arrived_shares = lax.all_to_all(
        shares, ("y", "zl"), split_axis=0, concat_axis=0, tiled=True
    )
    return finish(arrived_shares)


def solution(mesh):
    fine = Mesh(
        mesh.devices.reshape(4, 4, 2, 4, 2), ("zh", "x", "core", "y", "zl")
    )
    node, ctrl = ("zh", "x", "core"), ("y", "zl")
    in_specs = (P(None, node), P(None, node), P(None, ctrl), P(ctrl, node))
    out_specs = P(None, node + ctrl)

    return jax.shard_map(
        per_device, mesh=fine, in_specs=in_specs, out_specs=out_specs, check_vma=False
    )
```

```python
import functools

import jax
import jax.numpy as jnp
from jax import lax
from jax.experimental import pallas as pl
from jax.experimental.pallas import tpu as pltpu
from jax.sharding import Mesh, PartitionSpec as P


support_radius = 0.12
stretch = 4.0 / support_radius
depth = 128
used = 40
span = 256
whole = pl.BlockSpec(memory_space=pltpu.VMEM)
params = pltpu.CompilerParams(vmem_limit_bytes=20 * 1024 * 1024)


def pieces_of(values):
    high = values.astype(jnp.bfloat16).astype(jnp.float32)
    rest = values - high
    middle = rest.astype(jnp.bfloat16).astype(jnp.float32)
    low = (rest - middle).astype(jnp.bfloat16).astype(jnp.float32)
    return high, middle, low


def write_features(xyz_ref, rows, is_node):
    count = xyz_ref.shape[1]
    place = (xyz_ref[...] - 0.5) * stretch
    norm = (
        place[0:1] * place[0:1] + place[1:2] * place[1:2] + place[2:3] * place[2:3]
    )
    parts = pieces_of(place)
    norm_parts = pieces_of(norm)
    ones = jnp.ones((3, count), jnp.float32)
    rows[...] = jnp.zeros_like(rows)
    for i in range(3):
        for j in range(3):
            k = 3 * (3 * i + j)
            rows[k : k + 3, :] = parts[i] if is_node else -2.0 * parts[j]
    norm_at, ones_at = (27, 30) if is_node else (30, 27)
    rows[ones_at : ones_at + 3, :] = ones
    for i in range(3):
        rows[norm_at + i : norm_at + i + 1, :] = norm_parts[i]


def wendland(squared):
    r4 = squared * lax.rsqrt(squared)
    remain = jnp.maximum(4.0 - r4, 0.0)
    remain2 = remain * remain
    return (remain2 * remain2 * (r4 + 1.0)).astype(jnp.bfloat16)


tile = 512


def block_scratch(nodes):
    return [
        pltpu.VMEM((nodes, span), jnp.float32),
        pltpu.VMEM((nodes, span), jnp.bfloat16),
    ]


def pulled_block(node_ref, ctrl_ref, sens_ref, block, squares, weights):
    columns = pl.ds(pl.multiple_of(block * span, span), span)
    tiles = node_ref.shape[0] // tile

    def square(i):
        at = slice(i * tile, (i + 1) * tile)
        product = jnp.dot(
            node_ref[at, :], ctrl_ref[:, columns], preferred_element_type=jnp.float32
        )
        squares[at, :] = jnp.maximum(product, 1e-30)

    def gather(i):
        at = slice(i * tile, (i + 1) * tile)
        return jnp.dot(
            sens_ref[:, at], weights[at, :], preferred_element_type=jnp.float32
        )

    total = None
    square(0)
    for i in range(tiles):
        if i + 1 < tiles:
            square(i + 1)
        at = slice(i * tile, (i + 1) * tile)
        weights[at, :] = wendland(squares[at, :])
        if i > 0:
            term = gather(i - 1)
            total = term if total is None else total + term
    last = gather(tiles - 1)
    total = last if total is None else total + last
    return total * (1.0 / 256.0)


def block_of(step):
    return lax.axis_index("core") * 4 + lax.bitwise_xor(lax.axis_index("x"), step)


def first_kernel(
    step, sens_in, node_in, ctrl_in, out_ref, node_ref, sens_ref, ctrl_ref, *scratch
):
    node_xyz, ctrl_xyz, node_rows, ctrl_rows, done, squares, weights = scratch
    copies = [
        pltpu.make_async_copy(source, target, done.at[i])
        for i, (source, target) in enumerate(
            ((node_in, node_xyz), (ctrl_in, ctrl_xyz), (sens_in, sens_ref))
        )
    ]
    for copy in copies:
        copy.start()
    node_ref[...] = jnp.zeros_like(node_ref)
    ctrl_ref[...] = jnp.zeros_like(ctrl_ref)
    copies[0].wait()
    write_features(node_xyz, node_rows, True)
    node_ref[:, 0:used] = node_rows[...].T.astype(jnp.bfloat16)
    copies[1].wait()
    write_features(ctrl_xyz, ctrl_rows, False)
    ctrl_ref[0:used, :] = ctrl_rows[...].astype(jnp.bfloat16)
    copies[2].wait()
    out_ref[...] = pulled_block(
        node_ref, ctrl_ref, sens_ref, block_of(step), squares, weights
    )


def pull_cost(nodes, blocks):
    return pl.CostEstimate(
        flops=blocks * span * nodes * 400,
        bytes_accessed=nodes * 448,
        transcendentals=blocks * span * nodes,
    )


def first_pull(step, sens, node_xyz, ctrl_xyz):
    rows, nodes = sens.shape
    ctrls = ctrl_xyz.shape[1]
    return pl.pallas_call(
        functools.partial(first_kernel, step),
        out_shape=[
            jax.ShapeDtypeStruct((rows, span), jnp.float32),
            jax.ShapeDtypeStruct((nodes, depth), jnp.bfloat16),
            jax.ShapeDtypeStruct(sens.shape, sens.dtype),
            jax.ShapeDtypeStruct((depth, ctrls), jnp.bfloat16),
        ],
        in_specs=[pl.BlockSpec(memory_space=pltpu.HBM)] * 3,
        out_specs=[whole] * 4,
        scratch_shapes=[
            pltpu.VMEM(node_xyz.shape, jnp.float32),
            pltpu.VMEM(ctrl_xyz.shape, jnp.float32),
            pltpu.VMEM((used, nodes), jnp.float32),
            pltpu.VMEM((used, ctrls), jnp.float32),
            pltpu.SemaphoreType.DMA((3,)),
        ]
        + block_scratch(nodes),
        cost_estimate=pull_cost(nodes, 1),
        compiler_params=params,
        name="first_pull",
    )(*(pltpu.with_memory_space_constraint(a, pltpu.HBM) for a in (sens, node_xyz, ctrl_xyz)))


def second_kernel(
    step, part_ref, node_xyz, sens_ref, ctrl_ref, out_ref, node_ref, node_rows, *scratch
):
    node_ref[...] = jnp.zeros_like(node_ref)
    write_features(node_xyz, node_rows, True)
    node_ref[:, 0:used] = node_rows[...].T.astype(jnp.bfloat16)
    total = pulled_block(node_ref, ctrl_ref, sens_ref, block_of(step), *scratch)
    out_ref[...] = total + part_ref[...]


def second_pull(step, part, node_xyz, sens, ctrl_feat):
    rows, nodes = sens.shape
    return pl.pallas_call(
        functools.partial(second_kernel, step),
        out_shape=[
            jax.ShapeDtypeStruct((rows, span), jnp.float32),
            jax.ShapeDtypeStruct((nodes, depth), jnp.bfloat16),
        ],
        in_specs=[whole] * 4,
        out_specs=[whole] * 2,
        scratch_shapes=[pltpu.VMEM((used, nodes), jnp.float32)] + block_scratch(nodes),
        cost_estimate=pull_cost(nodes, 1),
        compiler_params=params,
        name="second_pull",
    )(part, node_xyz, sens, ctrl_feat)


def pull_kernel(step, node_a, sens_a, node_b, sens_b, ctrl_ref, out_ref, *scratch):
    block = block_of(step)
    total = pulled_block(node_a, ctrl_ref, sens_a, block, *scratch[:2])
    out_ref[...] = total + pulled_block(node_b, ctrl_ref, sens_b, block, *scratch[2:])


def pull(step, *prepared):
    rows, nodes = prepared[1].shape
    return pl.pallas_call(
        functools.partial(pull_kernel, step),
        out_shape=jax.ShapeDtypeStruct((rows, span), jnp.float32),
        in_specs=[whole] * len(prepared),
        out_specs=whole,
        scratch_shapes=block_scratch(nodes) * 2,
        cost_estimate=pull_cost(nodes, 2),
        compiler_params=params,
        name="pull",
    )(*prepared)


def product_kernel(order, *refs):
    blocks, inverse_ref, out_ref = refs[:-2], refs[-2], refs[-1]
    core = lax.axis_index("core")
    x = lax.axis_index("x")
    total = None
    for i, half in enumerate((core, 1 - core)):
        for joined, by in zip(blocks, order):
            at = pl.multiple_of((half * 4 + lax.bitwise_xor(x, by)) * span, span)
            block = joined[:, i * span : (i + 1) * span]
            term = jnp.dot(
                block,
                inverse_ref[pl.ds(at, span), :],
                preferred_element_type=jnp.float32,
            )
            total = term if total is None else total + term
    shares, rows, lanes = out_ref.shape
    width = lanes // 2
    for j in range(shares):
        share = total[:, j * width : (j + 1) * width]
        out_ref[j] = jnp.concatenate([share[:rows], share[rows:]], axis=1).astype(
            out_ref.dtype
        )


def product(order, blocks, inverse, shares):
    rows, width = blocks[0].shape[0], inverse.shape[1] // shares
    return pl.pallas_call(
        functools.partial(product_kernel, order),
        out_shape=jax.ShapeDtypeStruct((shares, rows // 2, 2 * width), jnp.bfloat16),
        in_specs=[whole] * (len(blocks) + 1),
        out_specs=whole,
        compiler_params=params,
        name="product",
    )(*blocks, inverse)


def finish_kernel(shares_ref, out_ref):
    total = shares_ref[0].astype(jnp.float32)
    for j in range(1, shares_ref.shape[0]):
        total = total + shares_ref[j].astype(jnp.float32)
    rows, lanes = total.shape
    turned = total.T
    out_ref[:, 0:rows] = turned[: lanes // 2]
    out_ref[:, rows:] = turned[lanes // 2 :]


def finish(shares):
    _, rows, lanes = shares.shape
    return pl.pallas_call(
        finish_kernel,
        out_shape=jax.ShapeDtypeStruct((lanes // 2, 2 * rows), jnp.float32),
        in_specs=[whole],
        out_specs=whole,
        compiler_params=params,
        name="finish",
    )(shares).T


def swapped(value, axis, by):
    size = lax.axis_size(axis)
    return lax.ppermute(value, axis, [(i, i ^ by) for i in range(size)])


def per_device(sensitivity, node_xyz, ctrl_xyz, inverse):
    other_sens = swapped(sensitivity, "core", 1)
    other_xyz = swapped(node_xyz, "core", 1)
    near, node_feat, sens, ctrl_feat = first_pull(1, sensitivity, node_xyz, ctrl_xyz)
    near, other_feat = second_pull(1, near, other_xyz, other_sens, ctrl_feat)
    prepared = (node_feat, sens, other_feat, other_sens, ctrl_feat)

    far = pull(2, *prepared)
    two = jnp.concatenate([near, far], axis=1).astype(jnp.bfloat16)
    two = swapped(two, "x", 1).astype(jnp.float32)
    right = pull(3, *prepared)
    right = (right + two[:, span:]).astype(jnp.bfloat16)
    right = swapped(right, "x", 3).astype(jnp.float32)
    summed = pull(0, *prepared)
    summed = summed + two[:, :span] + right

    low = summed.astype(jnp.bfloat16)
    for by in (2, 1, 3):
        summed = summed + swapped(low, "zh", by).astype(jnp.float32)
    mine = summed.astype(jnp.bfloat16)

    order = (2, 1, 3)
    both = jnp.concatenate([mine, swapped(mine, "core", 1)], axis=1)
    along_x = [both] + [swapped(both, "x", by) for by in order]
    shares = product((0,) + order, along_x, inverse, 8)
    arrived_shares = lax.all_to_all(
        shares, ("y", "zl"), split_axis=0, concat_axis=0, tiled=True
    )
    return finish(arrived_shares)


def solution(mesh):
    fine = Mesh(
        mesh.devices.reshape(4, 4, 2, 4, 2), ("zh", "x", "core", "y", "zl")
    )
    node, ctrl = ("zh", "x", "core"), ("y", "zl")
    in_specs = (P(None, node), P(None, node), P(None, ctrl), P(ctrl, node))
    out_specs = P(None, node + ctrl)

    return jax.shard_map(
        per_device, mesh=fine, in_specs=in_specs, out_specs=out_specs, check_vma=False
    )
```
